512 devices in a mesh: view: 32 (over x, z), slab: 16 (over y, core).
Axes of the slice: x: 4, y: 8, z: 8, core: 2. Of those that a mesh axis runs over, the one named last changes fastest.
Arguments:
- leaf_coeffs: float32 [64, 256, 768], P('view', 'slab'), may hold values from -6 to 6
- measured: float32 [64, 256, 768], P('view', 'slab'), may hold values from -6 to 6
- ray_weight: float32 [64, 256, 768], P('view', 'slab'), may hold values from 0.25 to 1
- cone_weight: float32 [64, 9], P('view'), may hold values from 0.1 to 0.5
- interp_weight: float32 [5, 2, 64, 4], replicated, may hold values from -2 to 2
- shift_offset: int32 [5, 2, 64], replicated, may hold values from -24 to 24
- source_view: int32 [5, 2, 64], replicated, may hold values from 0 to 1
Outputs:
- residual: float32 [64, 256, 768], P('view', 'slab')
- updated: float32 [64, 256, 768], P('view', 'slab')
The draws below stay inside these ranges and needn't reach their ends.
Inputs may be any that keep to these rules, and one draw needn't show every extreme that they name: source_view[l, c, v] is a view row within the supplying block.
All inputs are finite; a program needn't handle non-finite values.
Results may differ from the reference program's by a relative error of at most 0.00012.
Values sent between devices are 32-bit elements; how exact they have to be, the bound alone decides.
A program may use at most 64 MiB of HBM per device.

```python
import math
import jax
import jax.numpy as jnp
from jax import lax

U = 768
Q = 2
TAPS = 4
REACH = 4
SHIFT = 24
LEVELS = 5
NVIEWS = 64
NZ = 256


def with_ends(entries, rng, smallest, largest):
    longest = entries.shape.index(max(entries.shape))
    spots = []
    for shift in (0, 1):
        where = [jax.random.randint(jax.random.fold_in(rng, axis), (), 0, length) for axis, length in enumerate(entries.shape)]
        where[longest] = (where[longest] + shift) % entries.shape[longest]
        spots.append(tuple(where))
    return entries.at[spots[0]].set(smallest).at[spots[1]].set(largest)


def levels(stream_key, shape, pieces, least, largest):
    def one(axis_at, shards_of):
        heights = jax.random.uniform(jax.random.fold_in(jax.random.fold_in(stream_key, 6), axis_at), (shards_of,), jnp.float32, least / len(pieces), largest / len(pieces))
        return jnp.repeat(jnp.exp(heights), shape[axis_at] // shards_of).reshape((-1,) + (1,) * (len(shape) - axis_at - 1))

    factor_of = one(*pieces[0])
    for cut in pieces[1:]:
        factor_of = factor_of * one(*cut)
    return factor_of


def scatter_about(stream_key, shape, deviation, most, pieces=(), held_as=jnp.bfloat16):
    entries = jax.random.normal(stream_key, shape, jnp.float32) * deviation
    if len(pieces) > 0:
        entries = levels(stream_key, shape, pieces, -0.22, 0.18) * entries
    return jnp.clip(entries, min=-most, max=most).astype(held_as)


def setup_inputs(seed: int = 0) -> dict:
    key_list = jax.random.split(jax.random.key(seed), 8)
    return {
        "leaf_coeffs": scatter_about(key_list[0], (NVIEWS, NZ, U), 1.0, 6.0, ((0, 32), (1, 16)), jnp.float32),
        "measured": scatter_about(key_list[1], (NVIEWS, NZ, U), 1.0, 6.0, ((0, 32), (1, 16)), jnp.float32),
        "ray_weight": jnp.clip(jnp.exp(math.log(1.0) - 1.3862944 * jax.random.uniform(key_list[2], (NVIEWS, NZ, U), jnp.float32) ** levels(key_list[2], (NVIEWS, NZ, U), ((0, 32), (1, 16)), -0.2, 0.2)), 0.25, 1.0),
        "cone_weight": jnp.clip(0.1 + 0.4 * jax.random.uniform(key_list[3], (NVIEWS, 2 * REACH + 1), jnp.float32) ** levels(key_list[3], (NVIEWS, 2 * REACH + 1), ((0, 32),), -0.2, 0.2), 0.1, 0.5),
        "interp_weight": scatter_about(key_list[4], (LEVELS, 2, NVIEWS, TAPS), 0.35, 2.0, (), jnp.float32),
        "shift_offset": with_ends(jax.random.randint(key_list[5], (LEVELS, 2, NVIEWS), 0 - SHIFT, SHIFT + 1), jax.random.fold_in(key_list[5], 1), 0 - SHIFT, SHIFT).astype(jnp.int32),
        "source_view": with_ends(jax.random.randint(key_list[6], (LEVELS, 2, NVIEWS), 0, Q), jax.random.fold_in(key_list[6], 1), 0, Q - 1).astype(jnp.int32),
    }


def slide_rows(whole_block, starts, columns):

    def single_row(row_block, begin_at):
        return lax.dynamic_slice_in_dim(row_block, begin_at, columns, 1)
    return jax.vmap(single_row)(whole_block, starts)

def split_level(current, level_index, interp_weight, shift_offset, source_view):
    stride = 2 ** level_index
    row_ids = jnp.arange(NVIEWS, dtype=jnp.int32)
    owner_device = row_ids // Q
    partner = owner_device + stride - 2 * stride * (owner_device // stride % 2)
    margin = SHIFT + TAPS
    combined = jnp.zeros(current.shape, jnp.float32)
    for channel in range(2):
        supplier = owner_device if channel == 0 else partner
        picked = current[(supplier * Q + source_view[level_index, channel]).astype(jnp.int32)]
        padded = jnp.pad(picked, ((0, 0), (0, 0), (margin, margin)))
        for tap_index in range(TAPS):
            starts = (shift_offset[level_index, channel] + tap_index + margin).astype(jnp.int32)
            shifted = slide_rows(padded, starts, U)
            combined = combined + interp_weight[level_index, channel, :, tap_index][:, None, None] * shifted
    return combined

def tilt_planes(current, cone_weight):
    padded = jnp.pad(current, ((0, 0), (REACH, REACH), (0, 0)))
    combined = jnp.zeros(current.shape, jnp.float32)
    for cone_index in range(2 * REACH + 1):
        combined = combined + cone_weight[:, cone_index][:, None, None] * padded[:, cone_index:cone_index + NZ]
    return combined

def reference(leaf_coeffs, measured, ray_weight, cone_weight, interp_weight, shift_offset, source_view):

    def project(coeffs):
        current = coeffs
        for level_index in range(LEVELS):
            current = split_level(current, level_index, interp_weight, shift_offset, source_view)
        return tilt_planes(current, cone_weight)
    projection, pullback = jax.vjp(project, leaf_coeffs)
    residual = measured - projection
    weighted = ray_weight * residual
    backprojected, = pullback(weighted)
    return (residual, leaf_coeffs + backprojected)
```

```python
import functools

import jax
import jax.numpy as jnp
from jax import lax
from jax.experimental import pallas as pl
from jax.experimental.pallas import tpu as pltpu
from jax.sharding import PartitionSpec as P

MESH = pl.DeviceIdType.MESH
F32 = jnp.float32
TAPS = 4
LEVELS = 5
REACH = 4
PLANES = 16
HALF = 16
ROWS = 2 * HALF
CHUNKS = 6
LANES = 128
RING = 8 * LANES
COLUMNS = CHUNKS * LANES
BIAS = (24, 24, 24, 24, 32)
BASE = (128, 104, 80, 56, 32, 0)
UNROLL = 4


def lanes():
    return lax.broadcasted_iota(jnp.int32, (8, LANES), 1)


def places():
    return lax.broadcasted_iota(jnp.int32, (8, LANES), 0) * LANES + lanes()


def ahead(x, k):
    r = pltpu.roll(x, LANES - k, 1)
    return jnp.where(lanes() < LANES - k, r, pltpu.roll(r, 7, 0))


def behind(x, k):
    r = pltpu.roll(x, k, 1)
    return jnp.where(lanes() >= k, r, pltpu.roll(r, 1, 0))


def ahead_by(x, m):
    r = pltpu.roll(x, lax.rem(LANES - m, LANES), 1)
    return jnp.where(lanes() < LANES - m, r, pltpu.roll(r, 7, 0))


def behind_by(x, m):
    r = pltpu.roll(x, m, 1)
    return jnp.where(lanes() >= m, r, pltpu.roll(r, 1, 0))


def within(x, level):
    p = places()
    keep = (p >= BASE[level]) & (p < BASE[level] + COLUMNS)
    return jnp.where(keep, x, 0.0)


def flipped(i, stride):
    return i + stride - 2 * stride * ((i // stride) % 2)


def make_taps(src, taps, shifted):
    def step(i, carry):
        for v in range(2):
            x = src[2 * i + v]
            taps[0, 2 * i + v] = x
            for k in range(1, TAPS):
                taps[k, 2 * i + v] = shifted(x, k)
        return carry

    lax.fori_loop(0, HALF, step, 0, unroll=UNROLL)


def body(
    leaf_hbm, meas_hbm, rayw_hbm, w_s, off_s, src_s, cone_s, res_hbm, upd_hbm,
    leaf_v, meas_v, rayw_v, res_v, upd_v,
    stage, x0, ring_a, ring_b, sib_f, sib_b, taps_a, taps_b, split,
    v_buf, w_buf, meas_t, rayw_t, res_t, cot, g5, back, u_buf,
    in_sem, out_sem, send_sem, recv_sem, sib_sem, halo_send, halo_recv,
):
    d = lax.axis_index("view")
    s = lax.axis_index("slab")
    hi = d // HALF
    lo = d % HALF
    c = s % 2
    slab_to = s - c + hi
    sibling = s + 1 - 2 * c
    other = s - 1 + 2 * c
    has_other = jnp.logical_and(other >= 0, other < 16)
    intra = hi == c

    loads = [
        pltpu.make_async_copy(a, b, in_sem.at[i])
        for i, (a, b) in enumerate(((leaf_hbm, leaf_v), (meas_hbm, meas_v), (rayw_hbm, rayw_v)))
    ]
    for load in loads:
        load.start()

    zero = jnp.zeros((8, LANES), F32)

    def clear(i, carry):
        x0[i] = zero
        g5[i] = zero
        return carry

    lax.fori_loop(0, ROWS, clear, 0, unroll=4)
    for i in range(2 * REACH):
        v_buf[i] = zero
        w_buf[i] = zero
        v_buf[2 * (REACH + PLANES) + i] = zero
        w_buf[2 * (REACH + PLANES) + i] = zero

    barrier = pltpu.get_barrier_semaphore()

    def greet(i, carry):
        to = (lo + i) % HALF

        @pl.when(jnp.logical_not(jnp.logical_and(intra, to == lo)))
        def _():
            pl.semaphore_signal(
                barrier, inc=1, device_id=(HALF * c + to, slab_to), device_id_type=MESH
            )

        return carry

    lax.fori_loop(0, HALF, greet, 0)
    pl.semaphore_signal(barrier, inc=1, device_id=(d, sibling), device_id_type=MESH)

    @pl.when(has_other)
    def _():
        pl.semaphore_signal(barrier, inc=1, device_id=(d, other), device_id_type=MESH)

    def rows_in(dst, src, j0):
        flat = dst.reshape(PLANES * 2 * 8, LANES)
        for v in range(2):
            for h in range(2):
                for j in range(CHUNKS):
                    flat[pl.ds(h * 128 + v * 8 + j0 + j, 8, stride=16), :] = src[
                        v, 8 * h : 8 * h + 8, LANES * j : LANES * (j + 1)
                    ]

    loads[0].wait()
    rows_in(stage, leaf_v, 1)

    pl.semaphore_wait(
        barrier, jnp.where(intra, HALF - 1, HALF) + 1 + jnp.where(has_other, 1, 0)
    )

    def exchange(phase, src, dst, dst_row, first, begin, count):
        def step(n, carry):
            i = begin + (lo + n) % count
            a = src.at[pl.ds(2 * i, 2), pl.ds(first, CHUNKS)]
            b = dst.at[pl.ds(dst_row, 2), pl.ds(first, CHUNKS)]
            own = jnp.logical_and(intra, i == lo)

            @pl.when(own)
            def _():
                pltpu.make_async_copy(a, b, recv_sem.at[phase]).start()

            @pl.when(jnp.logical_not(own))
            def _():
                pltpu.make_async_remote_copy(
                    src_ref=a, dst_ref=b, send_sem=send_sem.at[phase], recv_sem=recv_sem.at[phase],
                    device_id=(HALF * c + i, slab_to), device_id_type=MESH,
                ).start()

            return carry

        lax.fori_loop(0, count, step, 0)

    def arrived(phase, dst, row, first):
        part = dst.at[pl.ds(row, ROWS), pl.ds(first, CHUNKS)]
        pltpu.make_async_copy(part, part, recv_sem.at[phase]).wait()

    def all_sent(phase, src, first):
        @pl.when(intra)
        def _():
            part = src.at[pl.ds(0, ROWS - 2), pl.ds(first, CHUNKS)]
            pltpu.make_async_copy(part, part, send_sem.at[phase]).wait()

        @pl.when(jnp.logical_not(intra))
        def _():
            part = src.at[pl.ds(0, ROWS), pl.ds(first, CHUNKS)]
            pltpu.make_async_copy(part, part, send_sem.at[phase]).wait()

    def to_sibling(n, src, dst):
        return pltpu.make_async_remote_copy(
            src_ref=src, dst_ref=dst, send_sem=sib_sem.at[n, 0], recv_sem=sib_sem.at[n, 1],
            device_id=(d, sibling), device_id_type=MESH,
        )

    exchange(0, stage, x0, 2 * lo, 1, 0, HALF)
    loads[1].wait()
    loads[2].wait()
    rows_in(meas_t, meas_v, 0)
    rows_in(rayw_t, rayw_v, 0)
    arrived(0, x0, 0, 1)

    def forward_term(level, channel, row, base, taps):
        src = base + src_s[level, channel, row]
        z = w_s[level, channel, 0, row] * taps[0, src]
        for k in range(1, TAPS):
            z = z + w_s[level, channel, k, row] * taps[k, src]
        return ahead_by(z, off_s[level, channel, row] + BIAS[level])

    first_row = ROWS * c
    cur = x0
    for level in range(4):
        nxt = (ring_a, ring_b)[level % 2]
        make_taps(cur, taps_a, ahead)

        def step(i, carry, level=level, nxt=nxt):
            far = flipped(i, 2**level)
            for v in range(2):
                row = first_row + 2 * i + v
                y = forward_term(level, 0, row, 2 * i, taps_a) + forward_term(
                    level, 1, row, 2 * far, taps_a
                )
                nxt[2 * i + v] = within(y, level + 1)
            return carry

        lax.fori_loop(0, HALF, step, 0, unroll=UNROLL)
        cur = nxt

    to_sib = to_sibling(0, cur, sib_f)
    to_sib.start()
    make_taps(cur, taps_a, ahead)
    to_sib.wait_recv()
    make_taps(sib_f, taps_b, ahead)

    def last(i, carry):
        for v in range(2):
            row = first_row + 2 * i + v
            y = forward_term(4, 0, row, 2 * i, taps_a) + forward_term(4, 1, row, 2 * i, taps_b)
            split[2 * i + v] = y
        return carry

    lax.fori_loop(0, HALF, last, 0, unroll=UNROLL)

    exchange(1, split, v_buf, 2 * (REACH + lo), 0, 0, HALF)
    arrived(1, v_buf, 2 * REACH, 0)

    low, high = 2 * REACH, 2 * PLANES

    def halo(n, buf):
        up = c == 0
        src = jnp.where(up, high, low)
        dst = jnp.where(up, 0, low + high)
        near = pltpu.make_async_remote_copy(
            src_ref=buf.at[pl.ds(src, 2 * REACH), pl.ds(0, CHUNKS)],
            dst_ref=buf.at[pl.ds(dst, 2 * REACH), pl.ds(0, CHUNKS)],
            send_sem=halo_send.at[n, 0], recv_sem=halo_recv.at[n, 0],
            device_id=(d, sibling), device_id_type=MESH,
        )
        far_src = jnp.where(up, low, high)
        far_dst = jnp.where(up, low + high, 0)
        far = pltpu.make_async_remote_copy(
            src_ref=buf.at[pl.ds(far_src, 2 * REACH), pl.ds(0, CHUNKS)],
            dst_ref=buf.at[pl.ds(far_dst, 2 * REACH), pl.ds(0, CHUNKS)],
            send_sem=halo_send.at[n, 1], recv_sem=halo_recv.at[n, 1],
            device_id=(d, other), device_id_type=MESH,
        )
        return near, far

    def halo_start(pair):
        @pl.when(has_other)
        def _():
            pair[1].start()

        pair[0].start()

    def halo_arrived(pair):
        pair[0].wait_recv()

        @pl.when(has_other)
        def _():
            pair[1].wait_recv()

    def halo_sent(pair):
        pair[0].wait_send()

        @pl.when(has_other)
        def _():
            pair[1].wait_send()

    halo_v = halo(0, v_buf)
    halo_start(halo_v)

    def tilt(z0, z1):
        for v in range(2):
            for z in range(z0, z1):
                acc = cone_s[v, 0] * v_buf[2 * z + v]
                for e in range(1, 2 * REACH + 1):
                    acc = acc + cone_s[v, e] * v_buf[2 * (z + e) + v]
                r = meas_t[2 * z + v] - acc
                res_t[2 * z + v] = r
                w_buf[2 * (z + REACH) + v] = rayw_t[2 * z + v] * r

    def tilt_back(z0, z1):
        for v in range(2):
            for z in range(z0, z1):
                acc = cone_s[v, 0] * w_buf[2 * (z + 2 * REACH) + v]
                for e in range(1, 2 * REACH + 1):
                    acc = acc + cone_s[v, e] * w_buf[2 * (z + 2 * REACH - e) + v]
                cot[2 * z + v] = acc

    tilt(REACH, PLANES - REACH)
    halo_arrived(halo_v)
    tilt(0, REACH)
    tilt(PLANES - REACH, PLANES)
    halo_w = halo(1, w_buf)
    halo_start(halo_w)
    tilt_back(REACH, PLANES - REACH)
    halo_arrived(halo_w)
    tilt_back(0, REACH)
    tilt_back(PLANES - REACH, PLANES)

    exchange(2, cot, g5, 2 * lo, 0, 0, HALF)

    def rows_out(dst, src, j0, plus=None):
        flat = src.reshape(PLANES * 2 * 8, LANES)
        for v in range(2):
            for h in range(2):
                for j in range(CHUNKS):
                    x = flat[pl.ds(h * 128 + v * 8 + j0 + j, 8, stride=16), :]
                    at = (v, slice(8 * h, 8 * h + 8), slice(LANES * j, LANES * (j + 1)))
                    dst[at] = x if plus is None else plus[at] + x

    rows_out(res_v, res_t, 0)
    res_out = pltpu.make_async_copy(res_v, res_hbm, out_sem.at[0])
    res_out.start()
    arrived(2, g5, 0, 0)

    to_sib_b = to_sibling(1, g5, sib_b)
    to_sib_b.start()

    def backward_term(level, channel, row, at, taps):
        z = w_s[level, channel, 0, row] * taps[0, at]
        for k in range(1, TAPS):
            z = z + w_s[level, channel, k, row] * taps[k, at]
        y = behind_by(z, off_s[level, channel, row] + BIAS[level])
        first = src_s[level, channel, row] == 0
        return jnp.where(first, y, 0.0), jnp.where(first, 0.0, y)

    def backward_block(level, i, far, near_row, far_row, near_taps, far_taps, dst):
        sums = [None, None]
        for v in range(2):
            for channel, row, at, taps in (
                (0, near_row + v, 2 * i + v, near_taps),
                (1, far_row + v, 2 * far + v, far_taps),
            ):
                parts = backward_term(level, channel, row, at, taps)
                sums = [p if q is None else q + p for q, p in zip(sums, parts)]
        for v in range(2):
            dst[2 * i + v] = within(sums[v], level)

    make_taps(g5, taps_a, behind)
    to_sib_b.wait_recv()
    make_taps(sib_b, taps_b, behind)
    far_first = ROWS - ROWS * c

    def last_back(i, carry):
        backward_block(
            4, i, i, first_row + 2 * i, far_first + 2 * i, taps_a, taps_b, ring_a_b(4)
        )
        return carry

    def ring_a_b(level):
        return back if level == 0 else (ring_a, ring_b)[level % 2]

    to_sib.wait_send()
    lax.fori_loop(0, HALF, last_back, 0, unroll=UNROLL)
    for level in range(3, -1, -1):
        make_taps(ring_a_b(level + 1), taps_a, behind)

        def step_back(i, carry, level=level):
            far = flipped(i, 2**level)
            backward_block(
                level, i, far, first_row + 2 * i, first_row + 2 * far, taps_a, taps_a,
                ring_a_b(level),
            )
            return carry

        lax.fori_loop(0, HALF, step_back, 0, unroll=UNROLL)

    exchange(3, back, u_buf, 2 * lo, 1, 0, HALF)
    arrived(3, u_buf, 0, 1)
    rows_out(upd_v, u_buf, 1, leaf_v)
    upd_out = pltpu.make_async_copy(upd_v, upd_hbm, out_sem.at[1])
    upd_out.start()
    all_sent(0, stage, 1)
    all_sent(1, split, 0)
    all_sent(2, cot, 0)
    all_sent(3, back, 1)
    to_sib_b.wait_send()
    halo_sent(halo_v)
    halo_sent(halo_w)
    res_out.wait()
    upd_out.wait()


def step(leaf_coeffs, measured, ray_weight, cone_weight, interp_weight, shift_offset, source_view):
    block = leaf_coeffs.shape
    natural = pltpu.VMEM(block, F32)
    rows = pltpu.VMEM((ROWS, 8, LANES), F32)
    taps = pltpu.VMEM((TAPS, ROWS, 8, LANES), F32)
    planes = pltpu.VMEM((2 * (PLANES + 2 * REACH), 8, LANES), F32)
    out = jax.ShapeDtypeStruct(block, F32)
    hbm = pl.BlockSpec(memory_space=pl.ANY)
    smem = pl.BlockSpec(memory_space=pltpu.SMEM)
    return pl.pallas_call(
        body,
        out_shape=(out, out),
        in_specs=[hbm] * 3 + [smem] * 4,
        out_specs=(hbm, hbm),
        scratch_shapes=[natural] * 5
        + [rows] * 6
        + [taps] * 2
        + [rows]
        + [planes] * 2
        + [rows] * 7
        + [
            pltpu.SemaphoreType.DMA((3,)),
            pltpu.SemaphoreType.DMA((2,)),
            pltpu.SemaphoreType.DMA((4,)),
            pltpu.SemaphoreType.DMA((4,)),
            pltpu.SemaphoreType.DMA((2, 2)),
            pltpu.SemaphoreType.DMA((2, 2)),
            pltpu.SemaphoreType.DMA((2, 2)),
        ],
        compiler_params=pltpu.CompilerParams(
            collective_id=0, has_side_effects=True, vmem_limit_bytes=32 << 20
        ),
    )(
        leaf_coeffs, measured, ray_weight,
        jnp.transpose(interp_weight, (0, 1, 3, 2)), shift_offset, source_view, cone_weight,
    )


def solution(mesh):
    in_specs = (
        P("view", "slab", None),
        P("view", "slab", None),
        P("view", "slab", None),
        P("view", None),
        P(),
        P(),
        P(),
    )
    out_specs = (P("view", "slab", None), P("view", "slab", None))
    return jax.shard_map(step, mesh=mesh, in_specs=in_specs, out_specs=out_specs, check_vma=False)
```

```python
import functools

import jax
import jax.numpy as jnp
from jax import lax
from jax.experimental import pallas as pl
from jax.experimental.pallas import tpu as pltpu
from jax.sharding import PartitionSpec as P

MESH = pl.DeviceIdType.MESH
F32 = jnp.float32
TAPS = 4
LEVELS = 5
REACH = 4
EXTRA = 2 * REACH
SLABS = 16
PLANES = 16
HALF = 16
ROWS = 2 * HALF
CHUNKS = 6
LANES = 128
RING = 8 * LANES
COLUMNS = CHUNKS * LANES
BIAS = (24, 24, 24, 24, 32)
BASE = (128, 104, 80, 56, 32, 0)
UNROLL = 16
VMEM_LIMIT = 60 << 20


def lanes():
    return lax.broadcasted_iota(jnp.int32, (8, LANES), 1)


def places():
    return lax.broadcasted_iota(jnp.int32, (8, LANES), 0) * LANES + lanes()


def ahead(x, k):
    r = pltpu.roll(x, LANES - k, 1)
    return jnp.where(lanes() < LANES - k, r, pltpu.roll(r, 7, 0))


def behind(x, k):
    r = pltpu.roll(x, k, 1)
    return jnp.where(lanes() >= k, r, pltpu.roll(r, 1, 0))


def ahead_by(x, m):
    r = pltpu.roll(x, lax.rem(LANES - m, LANES), 1)
    return jnp.where(lanes() < LANES - m, r, pltpu.roll(r, 7, 0))


def behind_by(x, m):
    r = pltpu.roll(x, m, 1)
    return jnp.where(lanes() >= m, r, pltpu.roll(r, 1, 0))


def within(x, level):
    p = places()
    keep = (p >= BASE[level]) & (p < BASE[level] + COLUMNS)
    return jnp.where(keep, x, 0.0)


def flipped(i, stride):
    return i + stride - 2 * stride * ((i // stride) % 2)


def make_taps(src, taps, shifted):
    def step(i, carry):
        for v in range(2):
            x = src[2 * i + v]
            taps[0, 2 * i + v] = x
            for k in range(1, TAPS):
                taps[k, 2 * i + v] = shifted(x, k)
        return carry

    lax.fori_loop(0, HALF, step, 0, unroll=UNROLL)


def body(
    leaf_hbm, meas_hbm, rayw_hbm, w_h, off_h, src_h, cone_h, res_hbm, upd_hbm,
    w_s, off_s, src_s, cone_s,
    leaf_v, meas_v, rayw_v, res_v, upd_v,
    stage, x0, ring_a, ring_b, sib_f, sib_b, taps_a, taps_b, split,
    v_buf, w_buf, mr, res_t, cot, g5, back, u_buf,
    in_sem, out_sem, send_sem, recv_sem, beside_send, sib_sem, halo_send, halo_recv,
):
    d = lax.axis_index("view")
    s = lax.axis_index("slab")
    hi = d // HALF
    lo = d % HALF
    c = s % 2
    slab_to = s - c + hi
    sibling = s + 1 - 2 * c
    other = s - 1 + 2 * c
    has_other = jnp.logical_and(other >= 0, other < 16)
    intra = hi == c

    zero = jnp.zeros((8, LANES), F32)
    for i in range(ROWS):
        x0[i] = zero
        g5[i] = zero

    barrier = pltpu.get_barrier_semaphore()
    for i in range(HALF):
        to = (lo + i + 1) % HALF

        @pl.when(jnp.logical_not(jnp.logical_and(intra, to == lo)))
        def _(to=to):
            pl.semaphore_signal(
                barrier, inc=1, device_id=(HALF * c + to, slab_to), device_id_type=MESH
            )

    pl.semaphore_signal(barrier, inc=1, device_id=(d, sibling), device_id_type=MESH)

    @pl.when(has_other)
    def _():
        pl.semaphore_signal(barrier, inc=1, device_id=(d, other), device_id_type=MESH)

    loads = [
        pltpu.make_async_copy(a, b, in_sem.at[i])
        for i, (a, b) in enumerate(
            (
                (leaf_hbm, leaf_v), (meas_hbm, meas_v), (rayw_hbm, rayw_v),
                (w_h, w_s), (off_h, off_s), (src_h, src_s), (cone_h, cone_s),
            )
        )
    ]
    for load in loads:
        load.start()

    @pl.when(s == 0)
    def _():
        for i in range(2 * EXTRA):
            v_buf[i] = zero
        for i in range(2 * REACH):
            mr[0, i] = zero
            mr[1, i] = zero

    @pl.when(s == SLABS - 1)
    def _():
        for i in range(2 * EXTRA):
            v_buf[2 * (EXTRA + PLANES) + i] = zero
        for i in range(2 * REACH):
            mr[0, 2 * (REACH + PLANES) + i] = zero
            mr[1, 2 * (REACH + PLANES) + i] = zero

    def rows_in(dst, src, j0, plane0=0):
        flat = dst.reshape(dst.shape[0] * 8, LANES)
        for v in range(2):
            for h in range(2):
                for j in range(CHUNKS):
                    flat[pl.ds(16 * plane0 + h * 128 + v * 8 + j0 + j, 8, stride=16), :] = src[
                        v, 8 * h : 8 * h + 8, LANES * j : LANES * (j + 1)
                    ]

    loads[0].wait()
    rows_in(stage, leaf_v, 1)

    pl.semaphore_wait(
        barrier, jnp.where(intra, HALF - 1, HALF) + 1 + jnp.where(has_other, 1, 0)
    )

    def exchange(phase, src, dst, dst_row, first):
        for n in range(HALF):
            i = (lo + n + 1) % HALF
            a = src.at[pl.ds(2 * i, 2), pl.ds(first, CHUNKS)]
            b = dst.at[pl.ds(dst_row, 2), pl.ds(first, CHUNKS)]
            remote = pltpu.make_async_remote_copy(
                src_ref=a, dst_ref=b, send_sem=send_sem.at[phase], recv_sem=recv_sem.at[phase],
                device_id=(HALF * c + i, slab_to), device_id_type=MESH,
            )
            if n < HALF - 1:
                remote.start()
                continue

            @pl.when(intra)
            def _(a=a, b=b):
                pltpu.make_async_copy(a, b, recv_sem.at[phase]).start()

            @pl.when(jnp.logical_not(intra))
            def _(remote=remote):
                remote.start()

    def arrived(phase, dst, row, first, rows=ROWS):
        part = dst.at[pl.ds(row, rows), pl.ds(first, CHUNKS)]
        pltpu.make_async_copy(part, part, recv_sem.at[phase]).wait()

    def all_sent(phase, src, first):
        @pl.when(intra)
        def _():
            part = src.at[pl.ds(0, ROWS - 2), pl.ds(first, CHUNKS)]
            pltpu.make_async_copy(part, part, send_sem.at[phase]).wait()

        @pl.when(jnp.logical_not(intra))
        def _():
            part = src.at[pl.ds(0, ROWS), pl.ds(first, CHUNKS)]
            pltpu.make_async_copy(part, part, send_sem.at[phase]).wait()

    def to_sibling(n, src, dst):
        return pltpu.make_async_remote_copy(
            src_ref=src, dst_ref=dst, send_sem=sib_sem.at[n, 0], recv_sem=sib_sem.at[n, 1],
            device_id=(d, sibling), device_id_type=MESH,
        )

    exchange(0, stage, x0, 2 * lo, 1)
    loads[1].wait()
    loads[2].wait()
    rows_in(mr.at[0], meas_v, 0, REACH)
    rows_in(mr.at[1], rayw_v, 0, REACH)
    low, high, above = 2 * REACH, 2 * PLANES, 2 * (PLANES + REACH)
    up = c == 0

    def edges(n, src, dst, to):
        return pltpu.make_async_remote_copy(
            src_ref=mr.at[:, pl.ds(src, 2 * REACH), pl.ds(0, CHUNKS)],
            dst_ref=mr.at[:, pl.ds(dst, 2 * REACH), pl.ds(0, CHUNKS)],
            send_sem=halo_send.at[n], recv_sem=halo_recv.at[n],
            device_id=(d, to), device_id_type=MESH,
        )

    near = edges(0, jnp.where(up, high, low), jnp.where(up, 0, above), sibling)
    far = edges(1, jnp.where(up, low, high), jnp.where(up, above, 0), other)
    near.start()

    @pl.when(has_other)
    def _():
        far.start()

    for load in loads[3:]:
        load.wait()
    arrived(0, x0, 0, 1)

    def forward_term(level, channel, row, base, taps):
        src = base + src_s[level, channel, row]
        z = w_s[level, channel, 0, row] * taps[0, src]
        for k in range(1, TAPS):
            z = z + w_s[level, channel, k, row] * taps[k, src]
        return ahead_by(z, off_s[level, channel, row] + BIAS[level])

    first_row = ROWS * c
    cur = x0
    for level in range(4):
        nxt = (ring_a, ring_b)[level % 2]
        make_taps(cur, taps_a, ahead)

        def step(i, carry, level=level, nxt=nxt):
            far = flipped(i, 2**level)
            for v in range(2):
                row = first_row + 2 * i + v
                y = forward_term(level, 0, row, 2 * i, taps_a) + forward_term(
                    level, 1, row, 2 * far, taps_a
                )
                nxt[2 * i + v] = within(y, level + 1)
            return carry

        lax.fori_loop(0, HALF, step, 0, unroll=UNROLL)
        cur = nxt

    to_sib = to_sibling(0, cur, sib_f)
    to_sib.start()
    make_taps(cur, taps_a, ahead)

    def own_part(i, carry):
        for v in range(2):
            split[2 * i + v] = forward_term(4, 0, first_row + 2 * i + v, 2 * i, taps_a)
        return carry

    lax.fori_loop(0, HALF, own_part, 0, unroll=UNROLL)
    to_sib.wait_recv()
    make_taps(sib_f, taps_b, ahead)

    def far_part(i, carry):
        for v in range(2):
            split[2 * i + v] += forward_term(4, 1, first_row + 2 * i + v, 2 * i, taps_b)
        return carry

    lax.fori_loop(0, HALF, far_part, 0, unroll=UNROLL)

    exchange(1, split, v_buf, 2 * (EXTRA + lo), 0)
    lower = lo < EXTRA
    slab_beside = jnp.where(lower, slab_to - 1, slab_to + 1)
    has_beside = jnp.logical_and(slab_beside >= 0, slab_beside < SLABS)
    beside_row = 2 * jnp.where(lower, EXTRA + PLANES + lo, EXTRA - PLANES + lo)

    @pl.when(has_beside)
    def _():
        for n in range(HALF):
            i = (lo + n) % HALF
            pltpu.make_async_remote_copy(
                src_ref=split.at[pl.ds(2 * i, 2), pl.ds(0, CHUNKS)],
                dst_ref=v_buf.at[pl.ds(beside_row, 2), pl.ds(0, CHUNKS)],
                send_sem=beside_send, recv_sem=recv_sem.at[1],
                device_id=(HALF * c + i, slab_beside), device_id_type=MESH,
            ).start()

    near.wait_recv()

    @pl.when(has_other)
    def _():
        far.wait_recv()

    inner = jnp.logical_and(s > 0, s < SLABS - 1)

    @pl.when(inner)
    def _():
        arrived(1, v_buf, 0, 0, 2 * (PLANES + 2 * EXTRA))

    @pl.when(jnp.logical_not(inner))
    def _():
        arrived(1, v_buf, 0, 0, 2 * (PLANES + EXTRA))

    for v in range(2):
        for z in range(PLANES + 2 * REACH):
            acc = cone_s[v, 0] * v_buf[2 * z + v]
            for e in range(1, 2 * REACH + 1):
                acc = acc + cone_s[v, e] * v_buf[2 * (z + e) + v]
            r = mr[0, 2 * z + v] - acc
            if REACH <= z < REACH + PLANES:
                res_t[2 * (z - REACH) + v] = r
            w_buf[2 * z + v] = mr[1, 2 * z + v] * r
    for v in range(2):
        for z in range(PLANES):
            acc = cone_s[v, 0] * w_buf[2 * (z + 2 * REACH) + v]
            for e in range(1, 2 * REACH + 1):
                acc = acc + cone_s[v, e] * w_buf[2 * (z + 2 * REACH - e) + v]
            cot[2 * z + v] = acc

    exchange(2, cot, g5, 2 * lo, 0)

    def rows_out(dst, src, j0, plus=None):
        flat = src.reshape(PLANES * 2 * 8, LANES)
        for v in range(2):
            for h in range(2):
                for j in range(CHUNKS):
                    x = flat[pl.ds(h * 128 + v * 8 + j0 + j, 8, stride=16), :]
                    at = (v, slice(8 * h, 8 * h + 8), slice(LANES * j, LANES * (j + 1)))
                    dst[at] = x if plus is None else plus[at] + x

    rows_out(res_v, res_t, 0)
    res_out = pltpu.make_async_copy(res_v, res_hbm, out_sem.at[0])
    res_out.start()
    arrived(2, g5, 0, 0)

    to_sib_b = to_sibling(1, g5, sib_b)
    to_sib_b.start()

    def backward_term(level, channel, row, at, taps):
        z = w_s[level, channel, 0, row] * taps[0, at]
        for k in range(1, TAPS):
            z = z + w_s[level, channel, k, row] * taps[k, at]
        y = behind_by(z, off_s[level, channel, row] + BIAS[level])
        first = src_s[level, channel, row] == 0
        return jnp.where(first, y, 0.0), jnp.where(first, 0.0, y)

    def backward_sums(level, terms, sums=(None, None)):
        for channel, row, at, taps in terms:
            parts = backward_term(level, channel, row, at, taps)
            sums = [p if q is None else q + p for q, p in zip(sums, parts)]
        return sums

    def ring(level):
        return back if level == 0 else (ring_a, ring_b)[level % 2]

    make_taps(g5, taps_a, behind)
    to_sib.wait_send()
    far_first = ROWS - ROWS * c

    def own_back(i, carry):
        sums = backward_sums(
            4, [(0, first_row + 2 * i + v, 2 * i + v, taps_a) for v in range(2)]
        )
        for v in range(2):
            ring(4)[2 * i + v] = sums[v]
        return carry

    lax.fori_loop(0, HALF, own_back, 0, unroll=UNROLL)
    to_sib_b.wait_recv()
    make_taps(sib_b, taps_b, behind)

    def far_back(i, carry):
        sums = backward_sums(
            4,
            [(1, far_first + 2 * i + v, 2 * i + v, taps_b) for v in range(2)],
            [ring(4)[2 * i + v] for v in range(2)],
        )
        for v in range(2):
            ring(4)[2 * i + v] = within(sums[v], 4)
        return carry

    lax.fori_loop(0, HALF, far_back, 0, unroll=UNROLL)
    for level in range(3, -1, -1):
        make_taps(ring(level + 1), taps_a, behind)

        def step_back(i, carry, level=level):
            far = flipped(i, 2**level)
            sums = backward_sums(
                level,
                [(0, first_row + 2 * i + v, 2 * i + v, taps_a) for v in range(2)]
                + [(1, first_row + 2 * far + v, 2 * far + v, taps_a) for v in range(2)],
            )
            for v in range(2):
                ring(level)[2 * i + v] = within(sums[v], level)
            return carry

        lax.fori_loop(0, HALF, step_back, 0, unroll=UNROLL)

    exchange(3, back, u_buf, 2 * lo, 1)
    arrived(3, u_buf, 0, 1)
    rows_out(upd_v, u_buf, 1, leaf_v)
    upd_out = pltpu.make_async_copy(upd_v, upd_hbm, out_sem.at[1])
    upd_out.start()
    all_sent(0, stage, 1)
    all_sent(1, split, 0)
    all_sent(2, cot, 0)
    all_sent(3, back, 1)
    to_sib_b.wait_send()
    near.wait_send()

    @pl.when(has_other)
    def _():
        far.wait_send()

    @pl.when(has_beside)
    def _():
        part = split.at[pl.ds(0, ROWS), pl.ds(0, CHUNKS)]
        pltpu.make_async_copy(part, part, beside_send).wait()

    res_out.wait()
    upd_out.wait()


def step(leaf_coeffs, measured, ray_weight, cone_weight, interp_weight, shift_offset, source_view):
    block = leaf_coeffs.shape
    natural = pltpu.VMEM(block, F32)
    rows = pltpu.VMEM((ROWS, 8, LANES), F32)
    taps = pltpu.VMEM((TAPS, ROWS, 8, LANES), F32)
    planes_v = pltpu.VMEM((2 * (PLANES + 2 * EXTRA), 8, LANES), F32)
    planes_w = pltpu.VMEM((2 * (PLANES + 2 * REACH), 8, LANES), F32)
    planes_mr = pltpu.VMEM((2, 2 * (PLANES + 2 * REACH), 8, LANES), F32)
    out = jax.ShapeDtypeStruct(block, F32)
    hbm = pl.BlockSpec(memory_space=pl.ANY)
    return pl.pallas_call(
        body,
        out_shape=(out, out),
        in_specs=[hbm] * 7,
        out_specs=(hbm, hbm),
        scratch_shapes=[
            pltpu.SMEM((LEVELS, 2, TAPS, 64), F32),
            pltpu.SMEM((LEVELS, 2, 64), jnp.int32),
            pltpu.SMEM((LEVELS, 2, 64), jnp.int32),
            pltpu.SMEM((2, 2 * REACH + 1), F32),
        ]
        + [natural] * 5
        + [rows] * 6
        + [taps] * 2
        + [rows]
        + [planes_v, planes_w, planes_mr]
        + [rows] * 5
        + [
            pltpu.SemaphoreType.DMA((7,)),
            pltpu.SemaphoreType.DMA((2,)),
            pltpu.SemaphoreType.DMA((4,)),
            pltpu.SemaphoreType.DMA((4,)),
            pltpu.SemaphoreType.DMA,
            pltpu.SemaphoreType.DMA((2, 2)),
            pltpu.SemaphoreType.DMA((2,)),
            pltpu.SemaphoreType.DMA((2,)),
        ],
        compiler_params=pltpu.CompilerParams(
            collective_id=0, has_side_effects=True, vmem_limit_bytes=VMEM_LIMIT
        ),
    )(
        leaf_coeffs, measured, ray_weight,
        jnp.transpose(interp_weight, (0, 1, 3, 2)), shift_offset, source_view, cone_weight,
    )


def solution(mesh):
    in_specs = (
        P("view", "slab", None),
        P("view", "slab", None),
        P("view", "slab", None),
        P("view", None),
        P(),
        P(),
        P(),
    )
    out_specs = (P("view", "slab", None), P("view", "slab", None))
    return jax.shard_map(step, mesh=mesh, in_specs=in_specs, out_specs=out_specs, check_vma=False)
```

```python
import functools

import jax
import jax.numpy as jnp
from jax import lax
from jax.experimental import pallas as pl
from jax.experimental.pallas import tpu as pltpu
from jax.sharding import PartitionSpec as P

MESH = pl.DeviceIdType.MESH
F32 = jnp.float32
TAPS = 4
LEVELS = 5
REACH = 4
EXTRA = 2 * REACH
SLABS = 16
PLANES = 16
HALF = 16
ROWS = 2 * HALF
CHUNKS = 6
LANES = 128
RING = 8 * LANES
COLUMNS = CHUNKS * LANES
BIAS = (24, 24, 24, 24, 32)
BASE = (128, 104, 80, 56, 32, 0)
UNROLL = 16
FAR_FIRST = tuple((a, b) for b in (4, 3, 5, 2, 6, 1, 7, 0) for a in (1, 0))
VMEM_LIMIT = 24 << 20


def lanes():
    return lax.broadcasted_iota(jnp.int32, (8, LANES), 1)


def places():
    return lax.broadcasted_iota(jnp.int32, (8, LANES), 0) * LANES + lanes()


def ahead(x, k):
    r = pltpu.roll(x, LANES - k, 1)
    return jnp.where(lanes() < LANES - k, r, pltpu.roll(r, 7, 0))


def behind(x, k):
    r = pltpu.roll(x, k, 1)
    return jnp.where(lanes() >= k, r, pltpu.roll(r, 1, 0))


def within(x, level):
    p = places()
    keep = (p >= BASE[level]) & (p < BASE[level] + COLUMNS)
    return jnp.where(keep, x, 0.0)


def flipped(i, stride):
    return i + stride - 2 * stride * ((i // stride) % 2)


def make_taps(src, taps, shifted):
    def step(i, carry):
        for v in range(2):
            x = src[2 * i + v]
            taps[0, 2 * i + v] = x
            for k in range(1, TAPS):
                taps[k, 2 * i + v] = shifted(x, k)
        return carry

    lax.fori_loop(0, HALF, step, 0, unroll=UNROLL)


def body(
    leaf_hbm, meas_hbm, rayw_hbm, w_h, off_h, src_h, cone_h, res_v, upd_v,
    w_s, off_s, src_s, cone_s,
    leaf_v, meas_v, rayw_v,
    stage, x0, ring_a, ring_b, sib_f, sib_b, taps_a, taps_b, split,
    w_t, m_t, s_t, w_far, m_far, s_far,
    v_buf, w_buf, mr, res_t, cot, g5, back, u_buf,
    in_sem, send_sem, recv_sem, beside_send, sib_sem, halo_send, halo_recv,
):
    d = lax.axis_index("view")
    s = lax.axis_index("slab")
    hi = d // HALF
    lo = d % HALF
    c = s % 2
    slab_to = s - c + hi
    sibling = s + 1 - 2 * c
    other = s - 1 + 2 * c
    has_other = jnp.logical_and(other >= 0, other < 16)
    intra = hi == c

    zero = jnp.zeros((8, LANES), F32)
    barrier = pltpu.get_barrier_semaphore()
    across, along = d // 8, d % 8

    def nth(n):
        a, b = FAR_FIRST[n]
        return 8 * ((across + a) % 2) + (along + b) % 8

    for n in range(HALF - 1):
        pl.semaphore_signal(
            barrier, inc=1, device_id=(HALF * c + nth(n), slab_to), device_id_type=MESH
        )

    @pl.when(jnp.logical_not(intra))
    def _():
        pl.semaphore_signal(
            barrier, inc=1, device_id=(HALF * c + lo, slab_to), device_id_type=MESH
        )

    pl.semaphore_signal(barrier, inc=1, device_id=(d, sibling), device_id_type=MESH)

    @pl.when(has_other)
    def _():
        pl.semaphore_signal(barrier, inc=1, device_id=(d, other), device_id_type=MESH)

    loads = [
        pltpu.make_async_copy(a, b, in_sem.at[i])
        for i, (a, b) in enumerate(
            (
                (leaf_hbm, leaf_v), (meas_hbm, meas_v), (rayw_hbm, rayw_v),
                (w_h, w_s), (off_h, off_s), (src_h, src_s), (cone_h, cone_s),
            )
        )
    ]
    for load in loads:
        load.start()

    for i in range(ROWS):
        x0[i, 0:1] = zero[0:1]
        x0[i, 7:8] = zero[0:1]
        g5[i, 6:8] = zero[0:2]

    @pl.when(s == 0)
    def _():
        for i in range(2 * EXTRA):
            v_buf[i] = zero
        for i in range(2 * REACH):
            mr[0, i] = zero
            mr[1, i] = zero

    @pl.when(s == SLABS - 1)
    def _():
        for i in range(2 * EXTRA):
            v_buf[2 * (EXTRA + PLANES) + i] = zero
        for i in range(2 * REACH):
            mr[0, 2 * (REACH + PLANES) + i] = zero
            mr[1, 2 * (REACH + PLANES) + i] = zero

    def rows_in(dst, src, j0, plane0=0):
        flat = dst.reshape(dst.shape[0] * 8, LANES)
        for v in range(2):
            for h in range(2):
                for j in range(CHUNKS):
                    flat[pl.ds(16 * plane0 + h * 128 + v * 8 + j0 + j, 8, stride=16), :] = src[
                        v, 8 * h : 8 * h + 8, LANES * j : LANES * (j + 1)
                    ]

    loads[0].wait()
    rows_in(stage, leaf_v, 1)

    pl.semaphore_wait(
        barrier, jnp.where(intra, HALF - 1, HALF) + 1 + jnp.where(has_other, 1, 0)
    )

    def exchange(phase, src, dst, dst_row, first):
        for n in range(HALF):
            i = nth(n)
            a = src.at[pl.ds(2 * i, 2), pl.ds(first, CHUNKS)]
            b = dst.at[pl.ds(dst_row, 2), pl.ds(first, CHUNKS)]
            remote = pltpu.make_async_remote_copy(
                src_ref=a, dst_ref=b, send_sem=send_sem.at[phase], recv_sem=recv_sem.at[phase],
                device_id=(HALF * c + i, slab_to), device_id_type=MESH,
            )
            if n < HALF - 1:
                remote.start()
                continue

            @pl.when(intra)
            def _(a=a, b=b):
                pltpu.make_async_copy(a, b, recv_sem.at[phase]).start()

            @pl.when(jnp.logical_not(intra))
            def _(remote=remote):
                remote.start()

    def arrived(phase, dst, row, first, rows=ROWS):
        part = dst.at[pl.ds(row, rows), pl.ds(first, CHUNKS)]
        pltpu.make_async_copy(part, part, recv_sem.at[phase]).wait()

    def all_sent(phase, src, first):
        @pl.when(intra)
        def _():
            part = src.at[pl.ds(0, ROWS - 2), pl.ds(first, CHUNKS)]
            pltpu.make_async_copy(part, part, send_sem.at[phase]).wait()

        @pl.when(jnp.logical_not(intra))
        def _():
            part = src.at[pl.ds(0, ROWS), pl.ds(first, CHUNKS)]
            pltpu.make_async_copy(part, part, send_sem.at[phase]).wait()

    def to_sibling(n, src, dst):
        return pltpu.make_async_remote_copy(
            src_ref=src, dst_ref=dst, send_sem=sib_sem.at[n, 0], recv_sem=sib_sem.at[n, 1],
            device_id=(d, sibling), device_id_type=MESH,
        )

    exchange(0, stage, x0, 2 * lo, 1)
    loads[1].wait()
    loads[2].wait()
    rows_in(mr.at[0], meas_v, 0, REACH)
    rows_in(mr.at[1], rayw_v, 0, REACH)
    low, high, above = 2 * REACH, 2 * PLANES, 2 * (PLANES + REACH)
    up = c == 0

    def edges(n, src, dst, to):
        return pltpu.make_async_remote_copy(
            src_ref=mr.at[:, pl.ds(src, 2 * REACH), pl.ds(0, CHUNKS)],
            dst_ref=mr.at[:, pl.ds(dst, 2 * REACH), pl.ds(0, CHUNKS)],
            send_sem=halo_send.at[n], recv_sem=halo_recv.at[n],
            device_id=(d, to), device_id_type=MESH,
        )

    near = edges(0, jnp.where(up, high, low), jnp.where(up, 0, above), sibling)
    far = edges(1, jnp.where(up, low, high), jnp.where(up, above, 0), other)
    near.start()

    @pl.when(has_other)
    def _():
        far.start()

    for load in loads[3:]:
        load.wait()
    first_row = ROWS * c
    far_first = ROWS - ROWS * c

    def spread(level, channel, row, at, w, m, sel):
        for k in range(TAPS):
            w[TAPS * at + k] = jnp.full((8, LANES), w_s[level, channel, k, row], F32)
        m[at] = jnp.full((8, LANES), off_s[level, channel, row], jnp.int32)
        sel[at] = jnp.full((8, LANES), src_s[level, channel, row], jnp.int32).astype(F32)

    def spread_rows(r, carry):
        for level in range(LEVELS):
            for channel in range(2):
                spread(
                    level, channel, first_row + r, ROWS * (2 * level + channel) + r, w_t, m_t, s_t
                )
        spread(LEVELS - 1, 1, far_first + r, r, w_far, m_far, s_far)
        return carry

    lax.fori_loop(0, ROWS, spread_rows, 0)
    arrived(0, x0, 0, 1)

    def forward_term(level, channel, r, base, taps):
        row, at = first_row + r, ROWS * (2 * level + channel) + r
        src = base + src_s[level, channel, row]
        z = w_t[TAPS * at] * taps[0, src]
        for k in range(1, TAPS):
            z = z + w_t[TAPS * at + k] * taps[k, src]
        by = off_s[level, channel, row] + BIAS[level]
        turned = pltpu.roll(z, lax.rem(LANES - by, LANES), 1)
        keep = (LANES - 1 - BIAS[level]) - lanes() >= m_t[at]
        return jnp.where(keep, turned, pltpu.roll(turned, 7, 0))

    cur = x0
    for level in range(4):
        nxt = (ring_a, ring_b)[level % 2]
        make_taps(cur, taps_a, ahead)

        def step(i, carry, level=level, nxt=nxt):
            far = flipped(i, 2**level)
            for v in range(2):
                r = 2 * i + v
                y = forward_term(level, 0, r, 2 * i, taps_a) + forward_term(
                    level, 1, r, 2 * far, taps_a
                )
                nxt[2 * i + v] = within(y, level + 1)
            return carry

        lax.fori_loop(0, HALF, step, 0, unroll=UNROLL)
        cur = nxt

    to_sib = to_sibling(0, cur, sib_f)
    to_sib.start()
    make_taps(cur, taps_a, ahead)

    def own_part(i, carry):
        for v in range(2):
            split[2 * i + v] = forward_term(4, 0, 2 * i + v, 2 * i, taps_a)
        return carry

    lax.fori_loop(0, HALF, own_part, 0, unroll=UNROLL)
    to_sib.wait_recv()
    make_taps(sib_f, taps_b, ahead)

    def far_part(i, carry):
        for v in range(2):
            split[2 * i + v] += forward_term(4, 1, 2 * i + v, 2 * i, taps_b)
        return carry

    lax.fori_loop(0, HALF, far_part, 0, unroll=UNROLL)

    lower = lo < EXTRA
    slab_beside = jnp.where(lower, slab_to - 1, slab_to + 1)
    has_beside = jnp.logical_and(slab_beside >= 0, slab_beside < SLABS)
    beside_row = 2 * jnp.where(lower, EXTRA + PLANES + lo, EXTRA - PLANES + lo)

    @pl.when(has_beside)
    def _():
        for n in range(HALF):
            i = nth(n)
            pltpu.make_async_remote_copy(
                src_ref=split.at[pl.ds(2 * i, 2), pl.ds(0, CHUNKS)],
                dst_ref=v_buf.at[pl.ds(beside_row, 2), pl.ds(0, CHUNKS)],
                send_sem=beside_send, recv_sem=recv_sem.at[1],
                device_id=(HALF * c + i, slab_beside), device_id_type=MESH,
            ).start()

    exchange(1, split, v_buf, 2 * (EXTRA + lo), 0)
    near.wait_recv()

    @pl.when(has_other)
    def _():
        far.wait_recv()

    inner = jnp.logical_and(s > 0, s < SLABS - 1)

    @pl.when(inner)
    def _():
        arrived(1, v_buf, 0, 0, 2 * (PLANES + 2 * EXTRA))

    @pl.when(jnp.logical_not(inner))
    def _():
        arrived(1, v_buf, 0, 0, 2 * (PLANES + EXTRA))

    for v in range(2):
        for z in range(PLANES + 2 * REACH):
            acc = cone_s[v, 0] * v_buf[2 * z + v]
            for e in range(1, 2 * REACH + 1):
                acc = acc + cone_s[v, e] * v_buf[2 * (z + e) + v]
            r = mr[0, 2 * z + v] - acc
            if REACH <= z < REACH + PLANES:
                res_t[2 * (z - REACH) + v] = r
            w_buf[2 * z + v] = mr[1, 2 * z + v] * r
    for v in range(2):
        for z in range(PLANES):
            acc = cone_s[v, 0] * w_buf[2 * (z + 2 * REACH) + v]
            for e in range(1, 2 * REACH + 1):
                acc = acc + cone_s[v, e] * w_buf[2 * (z + 2 * REACH - e) + v]
            cot[2 * z + v] = acc

    exchange(2, cot, g5, 2 * lo, 0)

    def rows_out(dst, src, j0, plus=None):
        flat = src.reshape(PLANES * 2 * 8, LANES)
        for v in range(2):
            for h in range(2):
                for j in range(CHUNKS):
                    x = flat[pl.ds(h * 128 + v * 8 + j0 + j, 8, stride=16), :]
                    at = (v, slice(8 * h, 8 * h + 8), slice(LANES * j, LANES * (j + 1)))
                    dst[at] = x if plus is None else plus[at] + x

    rows_out(res_v, res_t, 0)
    arrived(2, g5, 0, 0)

    to_sib_b = to_sibling(1, g5, sib_b)
    to_sib_b.start()

    def backward_term(level, channel, r, taps, tables=None):
        w, m, sel = tables or (w_t, m_t, s_t)
        at = r if tables else ROWS * (2 * level + channel) + r
        row = (far_first if tables else first_row) + r
        z = w[TAPS * at] * taps[0, r]
        for k in range(1, TAPS):
            z = z + w[TAPS * at + k] * taps[k, r]
        by = off_s[level, channel, row] + BIAS[level]
        turned = pltpu.roll(z, by, 1)
        y = jnp.where(lanes() - BIAS[level] >= m[at], turned, pltpu.roll(turned, 1, 0))
        second = y * sel[at]
        return y - second, second

    def backward_sums(level, terms, sums=(None, None)):
        for term in terms:
            parts = backward_term(level, *term)
            sums = [p if q is None else q + p for q, p in zip(sums, parts)]
        return sums

    def ring(level):
        return back if level == 0 else (ring_a, ring_b)[level % 2]

    make_taps(g5, taps_a, behind)
    to_sib.wait_send()

    def own_back(i, carry):
        sums = backward_sums(
            4, [(0, 2 * i + v, taps_a) for v in range(2)]
        )
        for v in range(2):
            ring(4)[2 * i + v] = sums[v]
        return carry

    lax.fori_loop(0, HALF, own_back, 0, unroll=UNROLL)
    to_sib_b.wait_recv()
    make_taps(sib_b, taps_b, behind)

    def far_back(i, carry):
        sums = backward_sums(
            4,
            [(1, 2 * i + v, taps_b, (w_far, m_far, s_far)) for v in range(2)],
            [ring(4)[2 * i + v] for v in range(2)],
        )
        for v in range(2):
            ring(4)[2 * i + v] = within(sums[v], 4)
        return carry

    lax.fori_loop(0, HALF, far_back, 0, unroll=UNROLL)
    for level in range(3, -1, -1):
        make_taps(ring(level + 1), taps_a, behind)

        def step_back(i, carry, level=level):
            far = flipped(i, 2**level)
            sums = backward_sums(
                level,
                [(0, 2 * i + v, taps_a) for v in range(2)]
                + [(1, 2 * far + v, taps_a) for v in range(2)],
            )
            for v in range(2):
                ring(level)[2 * i + v] = within(sums[v], level)
            return carry

        lax.fori_loop(0, HALF, step_back, 0, unroll=UNROLL)

    exchange(3, back, u_buf, 2 * lo, 1)
    arrived(3, u_buf, 0, 1)
    rows_out(upd_v, u_buf, 1, leaf_v)
    all_sent(0, stage, 1)
    all_sent(1, split, 0)
    all_sent(2, cot, 0)
    all_sent(3, back, 1)
    to_sib_b.wait_send()
    near.wait_send()

    @pl.when(has_other)
    def _():
        far.wait_send()

    @pl.when(has_beside)
    def _():
        part = split.at[pl.ds(0, ROWS), pl.ds(0, CHUNKS)]
        pltpu.make_async_copy(part, part, beside_send).wait()


def step(leaf_coeffs, measured, ray_weight, cone_weight, interp_weight, shift_offset, source_view):
    block = leaf_coeffs.shape
    natural = pltpu.VMEM(block, F32)
    rows = pltpu.VMEM((ROWS, 8, LANES), F32)
    taps = pltpu.VMEM((TAPS, ROWS, 8, LANES), F32)
    planes_v = pltpu.VMEM((2 * (PLANES + 2 * EXTRA), 8, LANES), F32)
    planes_w = pltpu.VMEM((2 * (PLANES + 2 * REACH), 8, LANES), F32)
    planes_mr = pltpu.VMEM((2, 2 * (PLANES + 2 * REACH), 8, LANES), F32)
    out = jax.ShapeDtypeStruct(block, F32)
    hbm = pl.BlockSpec(memory_space=pl.ANY)
    operands = (
        leaf_coeffs, measured, ray_weight,
        jnp.transpose(interp_weight, (0, 1, 3, 2)), shift_offset, source_view, cone_weight,
    )
    res, upd = pl.pallas_call(
        body,
        out_shape=(out, out),
        in_specs=[hbm] * 7,
        out_specs=(pl.BlockSpec(memory_space=pltpu.VMEM),) * 2,
        scratch_shapes=[
            pltpu.SMEM((LEVELS, 2, TAPS, 64), F32),
            pltpu.SMEM((LEVELS, 2, 64), jnp.int32),
            pltpu.SMEM((LEVELS, 2, 64), jnp.int32),
            pltpu.SMEM((2, 2 * REACH + 1), F32),
        ]
        + [natural] * 3
        + [rows] * 6
        + [taps] * 2
        + [rows]
        + [
            pltpu.VMEM((2 * LEVELS * ROWS * TAPS, 8, LANES), F32),
            pltpu.VMEM((2 * LEVELS * ROWS, 8, LANES), jnp.int32),
            pltpu.VMEM((2 * LEVELS * ROWS, 8, LANES), F32),
            pltpu.VMEM((ROWS * TAPS, 8, LANES), F32),
            pltpu.VMEM((ROWS, 8, LANES), jnp.int32),
            pltpu.VMEM((ROWS, 8, LANES), F32),
        ]
        + [planes_v, planes_w, planes_mr]
        + [rows] * 5
        + [
            pltpu.SemaphoreType.DMA((7,)),
            pltpu.SemaphoreType.DMA((4,)),
            pltpu.SemaphoreType.DMA((4,)),
            pltpu.SemaphoreType.DMA,
            pltpu.SemaphoreType.DMA((2, 2)),
            pltpu.SemaphoreType.DMA((2,)),
            pltpu.SemaphoreType.DMA((2,)),
        ],
        compiler_params=pltpu.CompilerParams(
            collective_id=0, has_side_effects=True, vmem_limit_bytes=VMEM_LIMIT
        ),
    )(*(pltpu.with_memory_space_constraint(x, pltpu.HBM) for x in operands))
    return pl.pallas_call(
        finish,
        out_shape=(out, out),
        in_specs=[hbm] * 2,
        out_specs=(hbm, hbm),
        scratch_shapes=[pltpu.SemaphoreType.DMA((2,))],
        compiler_params=pltpu.CompilerParams(vmem_limit_bytes=1 << 20),
    )(res, upd)


def finish(res, upd, res_hbm, upd_hbm, sem):
    copies = [
        pltpu.make_async_copy(a, b, sem.at[i])
        for i, (a, b) in enumerate(((res, res_hbm), (upd, upd_hbm)))
    ]
    for copy in copies:
        copy.start()
    for copy in copies:
        copy.wait()


def solution(mesh):
    in_specs = (
        P("view", "slab", None),
        P("view", "slab", None),
        P("view", "slab", None),
        P("view", None),
        P(),
        P(),
        P(),
    )
    out_specs = (P("view", "slab", None), P("view", "slab", None))
    return jax.shard_map(step, mesh=mesh, in_specs=in_specs, out_specs=out_specs, check_vma=False)
```

```python
import functools

import jax
import jax.numpy as jnp
from jax import lax
from jax.experimental import pallas as pl
from jax.experimental.pallas import tpu as pltpu
from jax.sharding import PartitionSpec as P

MESH = pl.DeviceIdType.MESH
F32 = jnp.float32
TAPS = 4
LEVELS = 5
REACH = 4
EXTRA = 2 * REACH
SLABS = 16
PLANES = 16
HALF = 16
ROWS = 2 * HALF
CHUNKS = 6
LANES = 128
RING = 8 * LANES
COLUMNS = CHUNKS * LANES
BIAS = (24, 24, 24, 24, 32)
BASE = (128, 104, 80, 56, 32, 0)
UNROLL = 16
FAR_FIRST = tuple((a, b) for b in (4, 3, 5, 2, 6, 1, 7, 0) for a in (1, 0))
VMEM_LIMIT = 24 << 20


def lanes():
    return lax.broadcasted_iota(jnp.int32, (8, LANES), 1)


def places():
    return lax.broadcasted_iota(jnp.int32, (8, LANES), 0) * LANES + lanes()


def ahead(x, k):
    return pltpu.roll(jnp.where(lanes() >= k, x, pltpu.roll(x, 7, 0)), LANES - k, 1)


def behind(x, k):
    return pltpu.roll(jnp.where(lanes() < LANES - k, x, pltpu.roll(x, 1, 0)), k, 1)


def within(x, level):
    p = places()
    keep = (p >= BASE[level]) & (p < BASE[level] + COLUMNS)
    return jnp.where(keep, x, 0.0)


def flipped(i, stride):
    return i + stride - 2 * stride * ((i // stride) % 2)


def make_taps(src, taps, shifted):
    def step(i, carry):
        for v in range(2):
            x = src[2 * i + v]
            taps[0, 2 * i + v] = x
            for k in range(1, TAPS):
                taps[k, 2 * i + v] = shifted(x, k)
        return carry

    lax.fori_loop(0, HALF, step, 0, unroll=UNROLL)


def body(
    leaf_hbm, meas_hbm, rayw_hbm, w_h, off_h, src_h, cone_h, res_v, upd_v,
    w_s, off_s, src_s, cone_s,
    leaf_v, meas_v, rayw_v,
    stage, x0, ring_a, ring_b, sib_f, sib_b, taps_a, taps_b, split,
    w_t, m_t, s_t, w_far, m_far, s_far,
    v_buf, w_buf, mr, res_t, cot, g5, back, u_buf,
    in_sem, send_sem, recv_sem, beside_send, sib_sem, halo_send, halo_recv,
):
    d = lax.axis_index("view")
    s = lax.axis_index("slab")
    hi = d // HALF
    lo = d % HALF
    c = s % 2
    slab_to = s - c + hi
    sibling = s + 1 - 2 * c
    other = s - 1 + 2 * c
    has_other = jnp.logical_and(other >= 0, other < 16)
    intra = hi == c

    zero = jnp.zeros((8, LANES), F32)
    barrier = pltpu.get_barrier_semaphore()
    across, along = d // 8, d % 8

    def nth(n):
        a, b = FAR_FIRST[n]
        return 8 * ((across + a) % 2) + (along + b) % 8

    for n in range(HALF - 1):
        pl.semaphore_signal(
            barrier, inc=1, device_id=(HALF * c + nth(n), slab_to), device_id_type=MESH
        )

    @pl.when(jnp.logical_not(intra))
    def _():
        pl.semaphore_signal(
            barrier, inc=1, device_id=(HALF * c + lo, slab_to), device_id_type=MESH
        )

    pl.semaphore_signal(barrier, inc=1, device_id=(d, sibling), device_id_type=MESH)

    @pl.when(has_other)
    def _():
        pl.semaphore_signal(barrier, inc=1, device_id=(d, other), device_id_type=MESH)

    loads = [
        pltpu.make_async_copy(a, b, in_sem.at[i])
        for i, (a, b) in enumerate(
            (
                (leaf_hbm, leaf_v), (meas_hbm, meas_v), (rayw_hbm, rayw_v),
                (w_h, w_s), (off_h, off_s), (src_h, src_s), (cone_h, cone_s),
            )
        )
    ]
    for load in loads:
        load.start()

    for i in range(ROWS):
        x0[i, 0:1] = zero[0:1]
        x0[i, 7:8] = zero[0:1]
        g5[i, 6:8] = zero[0:2]

    @pl.when(s == 0)
    def _():
        for i in range(2 * EXTRA):
            v_buf[i] = zero
        for i in range(2 * REACH):
            mr[0, i] = zero
            mr[1, i] = zero

    @pl.when(s == SLABS - 1)
    def _():
        for i in range(2 * EXTRA):
            v_buf[2 * (EXTRA + PLANES) + i] = zero
        for i in range(2 * REACH):
            mr[0, 2 * (REACH + PLANES) + i] = zero
            mr[1, 2 * (REACH + PLANES) + i] = zero

    def rows_in(dst, src, j0, plane0=0):
        flat = dst.reshape(dst.shape[0] * 8, LANES)
        for v in range(2):
            for h in range(2):
                for j in range(CHUNKS):
                    flat[pl.ds(16 * plane0 + h * 128 + v * 8 + j0 + j, 8, stride=16), :] = src[
                        v, 8 * h : 8 * h + 8, LANES * j : LANES * (j + 1)
                    ]

    loads[0].wait()
    rows_in(stage, leaf_v, 1)

    pl.semaphore_wait(
        barrier, jnp.where(intra, HALF - 1, HALF) + 1 + jnp.where(has_other, 1, 0)
    )

    def exchange(phase, src, dst, dst_row, first):
        for n in range(HALF):
            i = nth(n)
            a = src.at[pl.ds(2 * i, 2), pl.ds(first, CHUNKS)]
            b = dst.at[pl.ds(dst_row, 2), pl.ds(first, CHUNKS)]
            remote = pltpu.make_async_remote_copy(
                src_ref=a, dst_ref=b, send_sem=send_sem.at[phase], recv_sem=recv_sem.at[phase],
                device_id=(HALF * c + i, slab_to), device_id_type=MESH,
            )
            if n < HALF - 1:
                remote.start()
                continue

            @pl.when(intra)
            def _(a=a, b=b):
                pltpu.make_async_copy(a, b, recv_sem.at[phase]).start()

            @pl.when(jnp.logical_not(intra))
            def _(remote=remote):
                remote.start()

    def arrived(phase, dst, row, first, rows=ROWS):
        part = dst.at[pl.ds(row, rows), pl.ds(first, CHUNKS)]
        pltpu.make_async_copy(part, part, recv_sem.at[phase]).wait()

    def all_sent(phase, src, first):
        @pl.when(intra)
        def _():
            part = src.at[pl.ds(0, ROWS - 2), pl.ds(first, CHUNKS)]
            pltpu.make_async_copy(part, part, send_sem.at[phase]).wait()

        @pl.when(jnp.logical_not(intra))
        def _():
            part = src.at[pl.ds(0, ROWS), pl.ds(first, CHUNKS)]
            pltpu.make_async_copy(part, part, send_sem.at[phase]).wait()

    def to_sibling(n, src, dst):
        return pltpu.make_async_remote_copy(
            src_ref=src, dst_ref=dst, send_sem=sib_sem.at[n, 0], recv_sem=sib_sem.at[n, 1],
            device_id=(d, sibling), device_id_type=MESH,
        )

    exchange(0, stage, x0, 2 * lo, 1)
    loads[1].wait()
    loads[2].wait()
    rows_in(mr.at[0], meas_v, 0, REACH)
    rows_in(mr.at[1], rayw_v, 0, REACH)
    low, high, above = 2 * REACH, 2 * PLANES, 2 * (PLANES + REACH)
    up = c == 0

    def edges(n, src, dst, to):
        return pltpu.make_async_remote_copy(
            src_ref=mr.at[:, pl.ds(src, 2 * REACH), pl.ds(0, CHUNKS)],
            dst_ref=mr.at[:, pl.ds(dst, 2 * REACH), pl.ds(0, CHUNKS)],
            send_sem=halo_send.at[n], recv_sem=halo_recv.at[n],
            device_id=(d, to), device_id_type=MESH,
        )

    near = edges(0, jnp.where(up, high, low), jnp.where(up, 0, above), sibling)
    far = edges(1, jnp.where(up, low, high), jnp.where(up, above, 0), other)
    near.start()

    @pl.when(has_other)
    def _():
        far.start()

    for load in loads[3:]:
        load.wait()
    first_row = ROWS * c
    far_first = ROWS - ROWS * c

    def spread(level, channel, row, at, w, m, sel):
        for k in range(TAPS):
            w[TAPS * at + k] = jnp.full((8, LANES), w_s[level, channel, k, row], F32)
        m[at] = jnp.full((8, LANES), off_s[level, channel, row], jnp.int32)
        sel[at] = jnp.full((8, LANES), src_s[level, channel, row], jnp.int32).astype(F32)

    def spread_rows(r, carry):
        for level in range(LEVELS):
            for channel in range(2):
                spread(
                    level, channel, first_row + r, ROWS * (2 * level + channel) + r, w_t, m_t, s_t
                )
        spread(LEVELS - 1, 1, far_first + r, r, w_far, m_far, s_far)
        return carry

    lax.fori_loop(0, ROWS, spread_rows, 0)
    arrived(0, x0, 0, 1)

    def forward_term(level, channel, r, base, taps):
        row, at = first_row + r, ROWS * (2 * level + channel) + r
        src = base + src_s[level, channel, row]
        z = w_t[TAPS * at] * taps[0, src]
        for k in range(1, TAPS):
            z = z + w_t[TAPS * at + k] * taps[k, src]
        by = off_s[level, channel, row] + BIAS[level]
        turned = pltpu.roll(z, lax.rem(LANES - by, LANES), 1)
        keep = (LANES - 1 - BIAS[level]) - lanes() >= m_t[at]
        return jnp.where(keep, turned, 0.0), jnp.where(keep, 0.0, turned)

    def forward_row(terms):
        here, above = terms[0]
        for a, b in terms[1:]:
            here, above = here + a, above + b
        return here + pltpu.roll(above, 7, 0)

    cur = x0
    for level in range(4):
        nxt = (ring_a, ring_b)[level % 2]
        make_taps(cur, taps_a, ahead)

        def step(i, carry, level=level, nxt=nxt):
            far = flipped(i, 2**level)
            for v in range(2):
                r = 2 * i + v
                y = forward_row([forward_term(level, 0, r, 2 * i, taps_a), forward_term(
                    level, 1, r, 2 * far, taps_a
                )])
                nxt[2 * i + v] = within(y, level + 1)
            return carry

        lax.fori_loop(0, HALF, step, 0, unroll=UNROLL)
        cur = nxt

    to_sib = to_sibling(0, cur, sib_f)
    to_sib.start()
    make_taps(cur, taps_a, ahead)

    def own_part(i, carry):
        for v in range(2):
            split[2 * i + v] = forward_row([forward_term(4, 0, 2 * i + v, 2 * i, taps_a)])
        return carry

    lax.fori_loop(0, HALF, own_part, 0, unroll=UNROLL)
    to_sib.wait_recv()
    make_taps(sib_f, taps_b, ahead)

    def far_part(i, carry):
        for v in range(2):
            split[2 * i + v] += forward_row([forward_term(4, 1, 2 * i + v, 2 * i, taps_b)])
        return carry

    lax.fori_loop(0, HALF, far_part, 0, unroll=UNROLL)

    lower = lo < EXTRA
    slab_beside = jnp.where(lower, slab_to - 1, slab_to + 1)
    has_beside = jnp.logical_and(slab_beside >= 0, slab_beside < SLABS)
    beside_row = 2 * jnp.where(lower, EXTRA + PLANES + lo, EXTRA - PLANES + lo)

    exchange(1, split, v_buf, 2 * (EXTRA + lo), 0)

    @pl.when(has_beside)
    def _():
        for n in range(HALF):
            i = nth(n)
            pltpu.make_async_remote_copy(
                src_ref=split.at[pl.ds(2 * i, 2), pl.ds(0, CHUNKS)],
                dst_ref=v_buf.at[pl.ds(beside_row, 2), pl.ds(0, CHUNKS)],
                send_sem=beside_send, recv_sem=recv_sem.at[1],
                device_id=(HALF * c + i, slab_beside), device_id_type=MESH,
            ).start()

    near.wait_recv()

    @pl.when(has_other)
    def _():
        far.wait_recv()

    inner = jnp.logical_and(s > 0, s < SLABS - 1)

    @pl.when(inner)
    def _():
        arrived(1, v_buf, 0, 0, 2 * (PLANES + 2 * EXTRA))

    @pl.when(jnp.logical_not(inner))
    def _():
        arrived(1, v_buf, 0, 0, 2 * (PLANES + EXTRA))

    for v in range(2):
        for z in range(PLANES + 2 * REACH):
            acc = cone_s[v, 0] * v_buf[2 * z + v]
            for e in range(1, 2 * REACH + 1):
                acc = acc + cone_s[v, e] * v_buf[2 * (z + e) + v]
            r = mr[0, 2 * z + v] - acc
            if REACH <= z < REACH + PLANES:
                res_t[2 * (z - REACH) + v] = r
            w_buf[2 * z + v] = mr[1, 2 * z + v] * r
    for v in range(2):
        for z in range(PLANES):
            acc = cone_s[v, 0] * w_buf[2 * (z + 2 * REACH) + v]
            for e in range(1, 2 * REACH + 1):
                acc = acc + cone_s[v, e] * w_buf[2 * (z + 2 * REACH - e) + v]
            cot[2 * z + v] = acc

    exchange(2, cot, g5, 2 * lo, 0)

    def rows_out(dst, src, j0, plus=None):
        flat = src.reshape(PLANES * 2 * 8, LANES)
        for v in range(2):
            for h in range(2):
                for j in range(CHUNKS):
                    x = flat[pl.ds(h * 128 + v * 8 + j0 + j, 8, stride=16), :]
                    at = (v, slice(8 * h, 8 * h + 8), slice(LANES * j, LANES * (j + 1)))
                    dst[at] = x if plus is None else plus[at] + x

    rows_out(res_v, res_t, 0)
    arrived(2, g5, 0, 0)

    to_sib_b = to_sibling(1, g5.at[pl.ds(0, ROWS)], sib_b)
    to_sib_b.start()

    def backward_term(level, channel, r, taps, tables=None):
        w, m, sel = tables or (w_t, m_t, s_t)
        at = r if tables else ROWS * (2 * level + channel) + r
        row = (far_first if tables else first_row) + r
        z = w[TAPS * at] * taps[0, r]
        for k in range(1, TAPS):
            z = z + w[TAPS * at + k] * taps[k, r]
        by = off_s[level, channel, row] + BIAS[level]
        turned = pltpu.roll(z, by, 1)
        y = jnp.where(lanes() - BIAS[level] >= m[at], turned, pltpu.roll(turned, 1, 0))
        second = y * sel[at]
        return y - second, second

    def backward_sums(level, terms, sums=(None, None)):
        for term in terms:
            parts = backward_term(level, *term)
            sums = [p if q is None else q + p for q, p in zip(sums, parts)]
        return sums

    def ring(level):
        return back if level == 0 else (ring_a, ring_b)[level % 2]

    make_taps(g5, taps_a, behind)
    to_sib.wait_send()

    def own_back(i, carry):
        sums = backward_sums(
            4, [(0, 2 * i + v, taps_a) for v in range(2)]
        )
        for v in range(2):
            ring(4)[2 * i + v] = sums[v]
        return carry

    lax.fori_loop(0, HALF, own_back, 0, unroll=UNROLL)
    to_sib_b.wait_recv()
    make_taps(sib_b, taps_b, behind)

    def far_back(i, carry):
        sums = backward_sums(
            4,
            [(1, 2 * i + v, taps_b, (w_far, m_far, s_far)) for v in range(2)],
            [ring(4)[2 * i + v] for v in range(2)],
        )
        for v in range(2):
            ring(4)[2 * i + v] = within(sums[v], 4)
        return carry

    lax.fori_loop(0, HALF, far_back, 0, unroll=UNROLL)
    for level in range(3, -1, -1):
        make_taps(ring(level + 1), taps_a, behind)

        def step_back(i, carry, level=level):
            far = flipped(i, 2**level)
            sums = backward_sums(
                level,
                [(0, 2 * i + v, taps_a) for v in range(2)]
                + [(1, 2 * far + v, taps_a) for v in range(2)],
            )
            for v in range(2):
                ring(level)[2 * i + v] = within(sums[v], level)
            return carry

        lax.fori_loop(0, HALF, step_back, 0, unroll=UNROLL)

    exchange(3, back, u_buf, 2 * lo, 1)
    arrived(3, u_buf, 0, 1)
    rows_out(upd_v, u_buf, 1, leaf_v)
    all_sent(0, stage, 1)
    all_sent(1, split, 0)
    all_sent(2, cot, 0)
    all_sent(3, back, 1)
    to_sib_b.wait_send()
    near.wait_send()

    @pl.when(has_other)
    def _():
        far.wait_send()

    @pl.when(has_beside)
    def _():
        part = split.at[pl.ds(0, ROWS), pl.ds(0, CHUNKS)]
        pltpu.make_async_copy(part, part, beside_send).wait()


def step(leaf_coeffs, measured, ray_weight, cone_weight, interp_weight, shift_offset, source_view):
    block = leaf_coeffs.shape
    natural = pltpu.VMEM(block, F32)
    rows = pltpu.VMEM((ROWS, 8, LANES), F32)
    rows_more = pltpu.VMEM((ROWS + 1, 8, LANES), F32)
    taps = pltpu.VMEM((TAPS, ROWS, 8, LANES), F32)
    planes_v = pltpu.VMEM((2 * (PLANES + 2 * EXTRA), 8, LANES), F32)
    planes_w = pltpu.VMEM((2 * (PLANES + 2 * REACH), 8, LANES), F32)
    planes_mr = pltpu.VMEM((2, 2 * (PLANES + 2 * REACH), 8, LANES), F32)
    out = jax.ShapeDtypeStruct(block, F32)
    hbm = pl.BlockSpec(memory_space=pl.ANY)
    operands = (
        leaf_coeffs, measured, ray_weight,
        jnp.transpose(interp_weight, (0, 1, 3, 2)), shift_offset, source_view, cone_weight,
    )
    res, upd = pl.pallas_call(
        body,
        out_shape=(out, out),
        in_specs=[hbm] * 7,
        out_specs=(pl.BlockSpec(memory_space=pltpu.VMEM),) * 2,
        scratch_shapes=[
            pltpu.SMEM((LEVELS, 2, TAPS, 64), F32),
            pltpu.SMEM((LEVELS, 2, 64), jnp.int32),
            pltpu.SMEM((LEVELS, 2, 64), jnp.int32),
            pltpu.SMEM((2, 2 * REACH + 1), F32),
        ]
        + [natural] * 3
        + [rows, rows_more]
        + [rows] * 4
        + [taps] * 2
        + [rows]
        + [
            pltpu.VMEM((2 * LEVELS * ROWS * TAPS, 8, LANES), F32),
            pltpu.VMEM((2 * LEVELS * ROWS, 8, LANES), jnp.int32),
            pltpu.VMEM((2 * LEVELS * ROWS, 8, LANES), F32),
            pltpu.VMEM((ROWS * TAPS, 8, LANES), F32),
            pltpu.VMEM((ROWS, 8, LANES), jnp.int32),
            pltpu.VMEM((ROWS, 8, LANES), F32),
        ]
        + [planes_v, planes_w, planes_mr]
        + [rows] * 2
        + [rows_more]
        + [rows] * 2
        + [
            pltpu.SemaphoreType.DMA((7,)),
            pltpu.SemaphoreType.DMA((4,)),
            pltpu.SemaphoreType.DMA((4,)),
            pltpu.SemaphoreType.DMA,
            pltpu.SemaphoreType.DMA((2, 2)),
            pltpu.SemaphoreType.DMA((2,)),
            pltpu.SemaphoreType.DMA((2,)),
        ],
        compiler_params=pltpu.CompilerParams(
            collective_id=0, has_side_effects=True, vmem_limit_bytes=VMEM_LIMIT
        ),
    )(*(pltpu.with_memory_space_constraint(x, pltpu.HBM) for x in operands))
    return pl.pallas_call(
        finish,
        out_shape=(out, out),
        in_specs=[hbm] * 2,
        out_specs=(hbm, hbm),
        scratch_shapes=[pltpu.SemaphoreType.DMA((2,))],
        compiler_params=pltpu.CompilerParams(vmem_limit_bytes=1 << 20),
    )(res, upd)


def finish(res, upd, res_hbm, upd_hbm, sem):
    copies = [
        pltpu.make_async_copy(a, b, sem.at[i])
        for i, (a, b) in enumerate(((res, res_hbm), (upd, upd_hbm)))
    ]
    for copy in copies:
        copy.start()
    for copy in copies:
        copy.wait()


def solution(mesh):
    in_specs = (
        P("view", "slab", None),
        P("view", "slab", None),
        P("view", "slab", None),
        P("view", None),
        P(),
        P(),
        P(),
    )
    out_specs = (P("view", "slab", None), P("view", "slab", None))
    return jax.shard_map(step, mesh=mesh, in_specs=in_specs, out_specs=out_specs, check_vma=False)
```
